128 devices in a mesh: row: 16 (over y, z), basis: 8 (over x, core).
Axes of the slice: x: 4, y: 4, z: 4, core: 2. Of those that a mesh axis runs over, the one named last changes fastest.
Arguments:
- design: float32 [15360, 40960], P('row', 'basis'), may hold values from -0.029646354 to 0.029646354
- targets: float32 [15360], P('row'), may hold values from -6 to 6
- counts: int32 [15360, 128], P('row'), may hold values from 0 to 3
- coefficients: float32 [40960, 128], P('basis'), may hold values from -6 to 6
- step_size: float32 [128], replicated, may hold values from 0.03 to 0.15
Outputs:
- fitted: float32 [40960, 128], P('basis')
- influence: float32 [15360, 128], P('row')
The draws below stay inside these ranges and needn't reach their ends.
All inputs are finite; a program needn't handle non-finite values.
Results may differ from the reference program's by a relative error of at most 0.00017.
Values sent between devices are 32-bit elements; how exact they have to be, the bound alone decides.
A program may use at most 128 MiB of HBM per device.

```python
import math
import jax
import jax.numpy as jnp
from jax import lax

BASIS = 40960
MEMBERS = 128
STEPS = 3
ROWS = 15360


def touch_ends(array, key, low, largest):
    dims = array.shape
    place = [jax.random.randint(jax.random.fold_in(key, axis), (), 0, dims[axis]) for axis in range(len(dims))]
    array = array.at[tuple(place)].set(low)
    longest = dims.index(max(dims))
    place[longest] = (place[longest] + 1) % dims[longest]
    return array.at[tuple(place)].set(largest)


def strengthened(array, rng, source, target, parts, factor):
    def block_of(dim):
        return (jnp.arange(array.shape[dim]) // (array.shape[dim] // parts)).reshape((-1,) + (1,) * (array.ndim - 1 - dim))

    first = jax.random.permutation(rng, parts)[block_of(target)]
    other_side = (block_of(target) + parts // 2) % parts
    return jnp.where((block_of(source) == first) | (block_of(source) == other_side), factor * array, array)


def steps_of(stream_key, shape, shards, low, top_value):
    def one(axis_at, parts):
        draws = jax.random.uniform(jax.random.fold_in(jax.random.fold_in(stream_key, 6), axis_at), (parts,), jnp.float32, low / len(shards), top_value / len(shards))
        return jnp.repeat(jnp.exp(draws), shape[axis_at] // parts).reshape((-1,) + (1,) * (len(shape) - axis_at - 1))

    gain = one(*shards[0])
    for cut in shards[1:]:
        gain = gain * one(*cut)
    return gain


def bell_draw(stream_key, dims, deviation, reach, shards=(), held_as=jnp.bfloat16):
    result = deviation * jax.random.normal(stream_key, dims, jnp.float32)
    if shards:
        result = result * steps_of(stream_key, dims, shards, -0.22, 0.18)
    return jnp.clip(result, -reach, reach).astype(held_as)


def noise_with(rng, extent, scale, most, split, heavy, dtype=jnp.bfloat16):
    entries = scale * jax.random.normal(rng, extent, jnp.float32)
    if split:
        entries = entries * steps_of(rng, extent, split, -0.22, 0.18)
    return jnp.clip(strengthened(entries, jax.random.fold_in(rng, 3), *heavy), -most, most).astype(dtype)


def setup_inputs(seed: int = 0) -> dict:
    splits = jax.random.split(jax.random.key(seed), 6)
    design = noise_with(splits[0], (ROWS, BASIS), (BASIS ** -0.5), 0.029646354, ((0, 16), (1, 8)), (0, 1, 16, 2.0), jnp.float32)
    targets = bell_draw(splits[1], (ROWS,), 1.0, 6.0, ((0, 16),), jnp.float32)
    counts = touch_ends(jax.random.randint(splits[2], (ROWS, MEMBERS), 0, 4), jax.random.fold_in(splits[2], 1), 0, 3).astype(jnp.int32)
    coefficients = bell_draw(splits[3], (BASIS, MEMBERS), 1.0, 6.0, ((0, 8),), jnp.float32)
    step_size = jnp.clip(jnp.exp(jax.random.uniform(splits[4], (MEMBERS,), jnp.float32, math.log(0.03), math.log(0.15))), 0.03, 0.15)
    return dict(design=design, targets=targets, counts=counts, coefficients=coefficients, step_size=step_size)


HIGH = lax.Precision.HIGHEST

def transposed(left, right):
    return lax.dot_general(left, right, (((0,), (0,)), ((), ())), precision=HIGH, preferred_element_type=jnp.float32)

def reference(design, targets, counts, coefficients, step_size):
    weights = counts.astype(jnp.float32)
    curvature = transposed(design * design, weights) + 0.01
    fitted = coefficients
    influence = jnp.zeros((design.shape[0], coefficients.shape[1]), jnp.float32)
    for step in range(STEPS):
        predicted = jnp.dot(design, fitted, precision=HIGH, preferred_element_type=jnp.float32)
        residual = predicted - targets[:, None]
        influence = weights * residual / jnp.sqrt(1.0 + residual * residual)
        gradient = transposed(design, influence)
        fitted = fitted - step_size[None, :] * gradient / curvature
    return (fitted, influence)
```

```python
import functools

import jax
import jax.numpy as jnp
from jax import lax
from jax.experimental import pallas as pl
from jax.experimental.pallas import tpu as pltpu
from jax.sharding import PartitionSpec as P

STEPS = 3
SIDE = 4
LOADS = 10
GROUPS = 2
MESH = pl.DeviceIdType.MESH
F32 = jnp.float32
BF16 = jnp.bfloat16


def dot(a, b, ca=1, cb=0):
    return lax.dot_general(a, b, (((ca,), (cb,)), ((), ())), preferred_element_type=F32)


def parts(x):
    high = x.astype(BF16)
    return high, (x - high.astype(F32)).astype(BF16)


def kernel(
    design, coef, counts, targets, step_size, fit_out, inf_out,
    raw, dh, dl, cin, kin, wt, wtb, acc, curve, icat,
    grad, fit, infl, pred, r1, s1, r2, r3, rate, c1, sc, c2,
    load_sem, in_sem, out_sem,
    p1s, p1r, p2s, p2r, p3s, p3r, p4s, p4r, x1s, x1r, x2s, x2r, k1s, k1r, k2s, k2r,
):
    rows, cols = raw.shape
    members = wt.shape[0]
    m = members // GROUPS
    quarter = cols // (2 * SIDE)
    half = cols // 2
    part = m // SIDE
    peers = lax.axis_size("basis")
    piece = m // peers
    row, me = lax.axis_index("row"), lax.axis_index("basis")
    y, z = row // SIDE, lax.rem(row, SIDE)

    def at_y(d):
        return (lax.rem(y + d, SIDE) * SIDE + z, me)

    def at_z(d):
        return (y * SIDE + lax.rem(z + d, SIDE), me)

    def at_b(k):
        return (row, lax.rem(me + k, peers))

    first, second = (at_y, at_z), (at_z, at_y)
    major, minor = (y, z), (z, y)

    def columns(h, q):
        return pl.ds(pl.multiple_of(h * half + q * quarter, 128), quarter)

    def share_rows(h, d=0):
        return pl.ds(pl.multiple_of(lax.rem(minor[h] + d, SIDE) * part, 8), part)

    def piece_rows(k=0):
        return pl.ds(pl.multiple_of(lax.rem(me + k, peers) * piece, 8), piece)

    def remote(src, dst, send, recv, to):
        return pltpu.make_async_remote_copy(
            src_ref=src, dst_ref=dst, send_sem=send, recv_sem=recv, device_id=to, device_id_type=MESH
        )

    width = cols // LOADS

    def load(i):
        c = pl.ds(pl.multiple_of(i * width, 128), width)
        return pltpu.make_async_copy(design.at[:, c], raw.at[:, c], load_sem.at[i])

    coef_in = pltpu.make_async_copy(coef, cin, in_sem.at[0])
    counts_in = pltpu.make_async_copy(counts, kin, in_sem.at[1])
    counts_in.start()
    coef_in.start()
    for i in range(LOADS):
        load(i).start()

    barrier = pltpu.get_barrier_semaphore()
    for d in range(1, SIDE):
        pl.semaphore_signal(barrier, inc=1, device_id=at_y(d), device_id_type=MESH)
        pl.semaphore_signal(barrier, inc=1, device_id=at_z(d), device_id_type=MESH)
    for k in range(1, peers):
        pl.semaphore_signal(barrier, inc=1, device_id=at_b(k), device_id_type=MESH)

    def send1(g, h, d):
        there = lax.rem(major[h] + d, SIDE)
        return remote(
            grad.at[g, :, columns(h, there)], r1.at[g, h, d - 1],
            p1s.at[g, h, d - 1], p1r.at[g, h, d - 1], first[h](d),
        )

    def send2(g, h, d):
        return remote(
            s1.at[g, h, share_rows(h, d)], r2.at[g, h, d - 1],
            p2s.at[g, h, d - 1], p2r.at[g, h, d - 1], second[h](d),
        )

    def send3(g, h, d):
        mine = fit.at[g, share_rows(h), columns(h, major[h])]
        return remote(mine, mine, p3s.at[g, h, d - 1], p3r.at[g, h, d - 1], second[h](d))

    def send4(g, h, d):
        mine = fit.at[g, :, columns(h, major[h])]
        return remote(mine, mine, p4s.at[g, h, d - 1], p4r.at[g, h, d - 1], first[h](d))

    def sendx1(g, k):
        return remote(
            pred.at[g, piece_rows(k)], r3.at[g, k - 1], x1s.at[g, k - 1], x1r.at[g, k - 1], at_b(k)
        )

    def sendx2(g, k):
        mine = infl.at[g, piece_rows()]
        return remote(mine, mine, x2s.at[g, k - 1], x2r.at[g, k - 1], at_b(k))

    def sendk1(h, d):
        there = lax.rem(major[h] + d, SIDE)
        return remote(
            curve.at[:, columns(h, there)], c1.at[h, d - 1],
            k1s.at[h, d - 1], k1r.at[h, d - 1], first[h](d),
        )

    def sendk2(h, d):
        return remote(
            sc.at[h, :, share_rows(h, d)], c2.at[h, d - 1],
            k2s.at[h, d - 1], k2r.at[h, d - 1], second[h](d),
        )

    def gradients(g):
        high, low = parts(infl[g])
        icat[0:m] = high
        icat[m:] = low

        def body(j, _):
            d = lax.rem(j + 1, SIDE)
            for h in range(2):
                c = columns(h, lax.rem(major[h] + d, SIDE))
                both = dot(icat[...], dh[:, c])
                grad[g, :, c] = both[:m] + both[m:] + dot(icat[0:m], dl[:, c])

            @pl.when(j < SIDE - 1)
            def _():
                for h in range(2):
                    send1(g, h, j + 1).start()

            return 0

        lax.fori_loop(0, SIDE, body, 0)

    def reduce1(g):
        for h in range(2):
            for d in range(1, SIDE):
                send1(g, h, d).wait_recv()
            s1[g, h] = (grad[g, :, columns(h, major[h])] + r1[g, h, 0]) + (r1[g, h, 1] + r1[g, h, 2])
            for d in range(1, SIDE):
                send2(g, h, d).start()
        for h in range(2):
            for d in range(1, SIDE):
                send1(g, h, d).wait_send()

    def update(g):
        for h in range(2):
            for d in range(1, SIDE):
                send2(g, h, d).wait_recv()
            total = (s1[g, h, share_rows(h)] + r2[g, h, 0]) + (r2[g, h, 1] + r2[g, h, 2])
            c = columns(h, major[h])
            fit[g, share_rows(h), c] = fit[g, share_rows(h), c] - total * rate[g, h]
            for d in range(1, SIDE):
                send3(g, h, d).start()
        for h in range(2):
            for d in range(1, SIDE):
                send2(g, h, d).wait_send()

    def spread(g):
        for h in range(2):
            for d in range(1, SIDE):
                send3(g, h, d).wait_recv()
            for d in range(1, SIDE):
                send4(g, h, d).start()
        for h in range(2):
            for d in range(1, SIDE):
                send3(g, h, d).wait_send()

    def predict(g, d):
        total = None
        for h in range(2):
            c = columns(h, lax.rem(major[h] + SIDE - d, SIDE))
            high, low = parts(fit[g, :, c])
            both = dot(jnp.concatenate([high, low], 0), dh[:, c], 1, 1)
            term = both[:m] + both[m:] + dot(high, dl[:, c], 1, 1)
            total = term if total is None else total + term
        return total

    def predict_own(g):
        pred[g] = predict(g, 0)

    def predict_rest(g):
        def body(d, _):
            for h in range(2):
                send4(g, h, d).wait_recv()
            pred[g] += predict(g, d)
            return 0

        lax.fori_loop(1, SIDE, body, 0)
        for h in range(2):
            for d in range(1, SIDE):
                send4(g, h, d).wait_send()

    def scatter_pred(g):
        for k in range(1, peers):
            sendx1(g, k).start()

    def influence(g):
        for k in range(1, peers):
            sendx1(g, k).wait_recv()
        total = pred[g, piece_rows()]
        for k in range(1, peers):
            total = total + r3[g, k - 1]
        residual = total - targets[...]
        w = wt[pl.ds(pl.multiple_of(g * m + me * piece, 8), piece)]
        infl[g, piece_rows()] = w * residual / jnp.sqrt(1.0 + residual * residual)
        for k in range(1, peers):
            sendx2(g, k).start()
        for k in range(1, peers):
            sendx1(g, k).wait_send()

    def gathered(g):
        for k in range(1, peers):
            sendx2(g, k).wait_recv()
        for k in range(1, peers):
            sendx2(g, k).wait_send()

    counts_in.wait()
    wt[...] = kin[...].astype(F32).T
    wtb[...] = wt[...].astype(BF16)
    coef_in.wait()
    acc[...] = jnp.zeros_like(acc)

    def first_chunk(i, _):
        load(i).wait()
        c = pl.ds(pl.multiple_of(i * width, 128), width)
        high, low = parts(raw[:, c])
        dh[:, c] = high
        dl[:, c] = low
        fh, fl = parts(cin[c, :])
        both = dot(high, jnp.concatenate([fh, fl], 1))
        acc[...] += both[:, :members] + both[:, members:] + dot(low, fh)
        return 0

    lax.fori_loop(0, LOADS, first_chunk, 0)
    flipped = acc[...].T
    for g in range(GROUPS):
        pred[g] = flipped[g * m : (g + 1) * m]
    pl.semaphore_wait(barrier, 2 * (SIDE - 1) + peers - 1)
    for g in range(GROUPS):
        scatter_pred(g)

    def curve_chunk(j, _):
        d = lax.rem(j + 1, SIDE)
        for h in range(2):
            c = columns(h, lax.rem(major[h] + d, SIDE))
            x = raw[:, c]
            high, low = parts(x * x)
            curve[:, c] = dot(wtb[...], high) + dot(wtb[...], low)

        @pl.when(j < SIDE - 1)
        def _():
            for h in range(2):
                sendk1(h, j + 1).start()

        return 0

    lax.fori_loop(0, 2, curve_chunk, 0)
    influence(0)
    lax.fori_loop(2, SIDE, curve_chunk, 0)
    for h in range(2):
        start = pl.multiple_of(h * half + major[h] * quarter, 128)
        own = cin[pl.ds(start, quarter), :].T
        for g in range(GROUPS):
            fit[g, :, columns(h, major[h])] = own[g * m : (g + 1) * m]

    def curve_sum():
        for h in range(2):
            for d in range(1, SIDE):
                sendk1(h, d).wait_recv()
            total = (curve[:, columns(h, major[h])] + c1[h, 0]) + (c1[h, 1] + c1[h, 2])
            for g in range(GROUPS):
                sc[h, g] = total[g * m : (g + 1) * m]
            for d in range(1, SIDE):
                sendk2(h, d).start()

    def curve_rate():
        for h in range(2):
            for d in range(1, SIDE):
                sendk2(h, d).wait_recv()
            for g in range(GROUPS):
                total = (sc[h, g, share_rows(h)] + c2[h, 0, g]) + (c2[h, 1, g] + c2[h, 2, g])
                mine = pl.ds(pl.multiple_of(g * m + minor[h] * part, 8), part)
                rate[g, h] = step_size[mine] / (total + 0.01)
        for h in range(2):
            for d in range(1, SIDE):
                sendk1(h, d).wait_send()
                sendk2(h, d).wait_send()

    def step(s, _):
        more = s < STEPS - 1
        gathered(0)
        gradients(0)
        pl.when(s == 0)(curve_sum)
        influence(1)
        reduce1(0)
        gathered(1)
        gradients(1)
        pl.when(s == 0)(curve_rate)
        update(0)
        spread(0)
        reduce1(1)
        pl.when(more)(lambda: predict_own(0))
        update(1)

        @pl.when(more)
        def _():
            predict_rest(0)
            scatter_pred(0)

        spread(1)

        @pl.when(more)
        def _():
            predict_own(1)
            influence(0)
            predict_rest(1)
            scatter_pred(1)

        return 0

    lax.fori_loop(0, STEPS, step, 0)

    inf_copy = pltpu.make_async_copy(infl, inf_out, in_sem.at[0])
    inf_copy.start()

    def out_copy(g, h, d):
        c = columns(h, lax.rem(major[h] + SIDE - d, SIDE))
        return pltpu.make_async_copy(fit.at[g, :, c], fit_out.at[g, :, c], out_sem.at[g, h, d])

    for g in range(GROUPS):
        for h in range(2):
            out_copy(g, h, 0).start()
            for d in range(1, SIDE):
                send4(g, h, d).wait_recv()
                out_copy(g, h, d).start()
    for g in range(GROUPS):
        for h in range(2):
            for d in range(1, SIDE):
                send4(g, h, d).wait_send()
            for d in range(SIDE):
                out_copy(g, h, d).wait()
    inf_copy.wait()


def shards(design, targets, counts, coefficients, step_size):
    rows, cols = design.shape
    members = coefficients.shape[1]
    m = members // GROUPS
    quarter = cols // (2 * SIDE)
    part = m // SIDE
    peers = lax.axis_size("basis")
    piece = m // peers
    vmem = pltpu.VMEM
    dma = pltpu.SemaphoreType.DMA
    gh = (GROUPS, 2, SIDE - 1)
    any_spec = pl.BlockSpec(memory_space=pl.ANY)
    vmem_spec = pl.BlockSpec(memory_space=pltpu.VMEM)
    fit, infl = pl.pallas_call(
        kernel,
        out_shape=(
            jax.ShapeDtypeStruct((GROUPS, m, cols), F32),
            jax.ShapeDtypeStruct((GROUPS, m, rows), F32),
        ),
        in_specs=[any_spec, any_spec, any_spec, vmem_spec, vmem_spec],
        out_specs=(any_spec, any_spec),
        scratch_shapes=[
            vmem((rows, cols), F32),
            vmem((rows, cols), BF16),
            vmem((rows, cols), BF16),
            vmem((cols, members), F32),
            vmem((rows, members), jnp.int32),
            vmem((members, rows), F32),
            vmem((members, rows), BF16),
            vmem((rows, members), F32),
            vmem((members, cols), F32),
            vmem((2 * m, rows), BF16),
            vmem((GROUPS, m, cols), F32),
            vmem((GROUPS, m, cols), F32),
            vmem((GROUPS, m, rows), F32),
            vmem((GROUPS, m, rows), F32),
            vmem((*gh, m, quarter), F32),
            vmem((GROUPS, 2, m, quarter), F32),
            vmem((*gh, part, quarter), F32),
            vmem((GROUPS, peers - 1, piece, rows), F32),
            vmem((GROUPS, 2, part, quarter), F32),
            vmem((2, SIDE - 1, members, quarter), F32),
            vmem((2, GROUPS, m, quarter), F32),
            vmem((2, SIDE - 1, GROUPS, part, quarter), F32),
            dma((LOADS,)),
            dma((2,)),
            dma((GROUPS, 2, SIDE)),
            *[dma(gh) for _ in range(8)],
            *[dma((GROUPS, peers - 1)) for _ in range(4)],
            *[dma((2, SIDE - 1)) for _ in range(4)],
        ],
        compiler_params=pltpu.CompilerParams(
            collective_id=0, has_side_effects=True, vmem_limit_bytes=60 * 2**20
        ),
    )(design, coefficients, counts, targets[None, :], step_size[:, None])
    return fit.reshape(members, cols).T, infl.reshape(members, rows).T


def solution(mesh):
    return jax.shard_map(
        shards,
        mesh=mesh,
        in_specs=(P("row", "basis"), P("row"), P("row", None), P("basis", None), P()),
        out_specs=(P("basis", None), P("row", None)),
        check_vma=False,
    )
```

```python
import functools

import jax
import jax.numpy as jnp
from jax import lax
from jax.experimental import pallas as pl
from jax.experimental.pallas import tpu as pltpu
from jax.sharding import PartitionSpec as P

STEPS = 3
SIDE = 4
LOADS = 10
GROUPS = 2
BLOCKS = (384, 256)
ORDER = (
    "AX3", "AG21", "AG11", "AG31", "BX2", "AG20", "AG01", "AG10", "AG30", "KKS0", "KKS1", "AP211", "AP201",
    "BX3", "BG20", "BG10", "BG30", "AG00", "AP210", "AP200", "BG21", "BG00", "BG11", "BG31", "KKR",
    "BP200", "BP210", "AP310", "AP300", "AP301", "AP311", "BG01", "BP201", "BP211", "BP310", "BP300",
    "AP410", "AP400", "AF00", "AP411", "BP301", "AP401", "BP311", "BP410", "AF01", "BP400", "BF00", "AF20",
    "AF10", "AF30", "AF21", "AF31", "BP401", "BP411", "AF11", "AX1", "BF01", "BF10", "BF30", "BF21",
    "BF11", "AX2", "BF31", "BF20", "BX1",
)
MESH = pl.DeviceIdType.MESH
F32 = jnp.float32
BF16 = jnp.bfloat16


def dot(a, b, ca=1, cb=0):
    return lax.dot_general(a, b, (((ca,), (cb,)), ((), ())), preferred_element_type=F32)


def far_first(n):
    return [k for k in (4, 5, 3, 2, 6, 1, 7) if k < n]


def parts(x):
    high = x.astype(BF16)
    return high, (x - high.astype(F32)).astype(BF16)


def kernel(
    design, coef, counts, targets, step_size, fit_out, inf_out,
    steps, raw, dh, dl, cin, kin, wt, wtb, acc, curve, icat,
    grad, fit, infl, pred, r1, s1, r2, r3, rate, c1, sc, c2,
    load_sem, in_sem, out_sem,
    p1s, p1r, p2s, p2r, p3s, p3r, p4s, p4r, x1s, x1r, x2s, x2r, k1s, k1r, k2s, k2r,
):
    rows, cols = raw.shape
    members = wt.shape[0]
    m = members // GROUPS
    quarter = cols // (2 * SIDE)
    half = cols // 2
    part = m // SIDE
    peers = lax.axis_size("basis")
    piece = m // peers
    row, me = lax.axis_index("row"), lax.axis_index("basis")
    y, z = row // SIDE, lax.rem(row, SIDE)

    def at_y(d):
        return (lax.rem(y + d, SIDE) * SIDE + z, me)

    def at_z(d):
        return (y * SIDE + lax.rem(z + d, SIDE), me)

    def at_b(k):
        return (row, lax.rem(me + k, peers))

    def major(h):
        return y + h * (z - y)

    def minor(h):
        return z + h * (y - z)

    def inside(b):
        return slice(sum(BLOCKS[:b]), sum(BLOCKS[: b + 1]))

    def columns(h, q, b=None):
        w = slice(0, quarter) if b is None else inside(b)
        return pl.ds(pl.multiple_of(h * half + q * quarter + w.start, 128), w.stop - w.start)

    def share_rows(h, d=0):
        return pl.ds(pl.multiple_of(lax.rem(minor(h) + d, SIDE) * part, 8), part)

    def piece_rows(k=0):
        return pl.ds(pl.multiple_of(lax.rem(me + k, peers) * piece, 8), piece)

    def remote(src, dst, send, recv, to):
        return pltpu.make_async_remote_copy(
            src_ref=src, dst_ref=dst, send_sem=send, recv_sem=recv, device_id=to, device_id_type=MESH
        )

    width = cols // LOADS

    def load(i):
        c = pl.ds(pl.multiple_of(i * width, 128), width)
        return pltpu.make_async_copy(design.at[:, c], raw.at[:, c], load_sem.at[i])

    coef_in = pltpu.make_async_copy(coef, cin, in_sem.at[0])
    counts_in = pltpu.make_async_copy(counts, kin, in_sem.at[1])
    counts_in.start()
    coef_in.start()
    for i in range(LOADS):
        load(i).start()

    barrier = pltpu.get_barrier_semaphore()
    for d in range(1, SIDE):
        pl.semaphore_signal(barrier, inc=1, device_id=at_y(d), device_id_type=MESH)
        pl.semaphore_signal(barrier, inc=1, device_id=at_z(d), device_id_type=MESH)
    for k in range(1, peers):
        pl.semaphore_signal(barrier, inc=1, device_id=at_b(k), device_id_type=MESH)

    def first(h, d):
        return (lax.rem(y + d * (1 - h), SIDE) * SIDE + lax.rem(z + d * h, SIDE), me)

    def second(h, d):
        return first(1 - h, d)

    def send1(g, h, d, b):
        c = columns(h, lax.rem(major(h) + d, SIDE), b)
        return remote(
            grad.at[g, :, c], r1.at[g, h, d - 1, :, inside(b)],
            p1s.at[g, h, d - 1, b], p1r.at[g, h, d - 1, b], first(h, d),
        )

    def send2(g, h, d, b):
        return remote(
            s1.at[g, h, share_rows(h, d), inside(b)], r2.at[g, h, d - 1, :, inside(b)],
            p2s.at[g, h, d - 1, b], p2r.at[g, h, d - 1, b], second(h, d),
        )

    def send3(g, h, d, b):
        mine = fit.at[g, share_rows(h), columns(h, major(h), b)]
        return remote(mine, mine, p3s.at[g, h, d - 1, b], p3r.at[g, h, d - 1, b], second(h, d))

    def send4(g, h, d, b):
        mine = fit.at[g, :, columns(h, major(h), b)]
        return remote(mine, mine, p4s.at[g, h, d - 1, b], p4r.at[g, h, d - 1, b], first(h, d))

    def sendx1(g, k):
        return remote(
            pred.at[g, piece_rows(k)], r3.at[g, k - 1], x1s.at[g, k - 1], x1r.at[g, k - 1], at_b(k)
        )

    def sendx2(g, k):
        mine = infl.at[g, piece_rows()]
        return remote(mine, mine, x2s.at[g, k - 1], x2r.at[g, k - 1], at_b(k))

    def sendk1(h, d):
        return remote(
            curve.at[:, columns(h, lax.rem(major(h) + d, SIDE))], c1.at[h, d - 1],
            k1s.at[h, d - 1], k1r.at[h, d - 1], first(h, d),
        )

    def sendk2(h, d):
        return remote(
            sc.at[h, :, share_rows(h, d)], c2.at[h, d - 1],
            k2s.at[h, d - 1], k2r.at[h, d - 1], second(h, d),
        )

    def gathered(g):
        for k in far_first(peers):
            sendx2(g, k).wait_recv()
        for k in far_first(peers):
            sendx2(g, k).wait_send()
        high, low = parts(infl[g])
        icat[g, 0:m] = high
        icat[g, m:] = low

    def gradients(g, d, b):
        def body(h, _):
            c = columns(h, lax.rem(major(h) + d, SIDE), b)
            both = dot(icat[g], dh[:, c])
            grad[g, :, c] = both[:m] + both[m:] + dot(icat[g, 0:m], dl[:, c])
            if d:
                send1(g, h, d, b).start()
            return 0

        lax.fori_loop(0, 2, body, 0)

    def reduce1(g, h, b):
        for d in range(1, SIDE):
            send1(g, h, d, b).wait_recv()
        w = inside(b)
        mine = grad[g, :, columns(h, major(h), b)]
        s1[g, h, :, w] = (mine + r1[g, h, 0, :, w]) + (r1[g, h, 1, :, w] + r1[g, h, 2, :, w])
        for d in (2, 1, 3):
            send2(g, h, d, b).start()

    def update(g, h, b):
        for d in range(1, SIDE):
            send2(g, h, d, b).wait_recv()
        w = inside(b)
        total = (s1[g, h, share_rows(h), w] + r2[g, h, 0, :, w]) + (r2[g, h, 1, :, w] + r2[g, h, 2, :, w])
        c = columns(h, major(h), b)
        fit[g, share_rows(h), c] = fit[g, share_rows(h), c] - total * rate[g, h, :, w]
        for d in (2, 1, 3):
            send3(g, h, d, b).start()
        for d in range(1, SIDE):
            send1(g, h, d, b).wait_send()

    def spread(g, h, b):
        for d in range(1, SIDE):
            send3(g, h, d, b).wait_recv()
        for d in (2, 1, 3):
            send4(g, h, d, b).start()
        for d in range(1, SIDE):
            send2(g, h, d, b).wait_send()

    def predict(g, d, b):
        if d == 0 and b == 0:
            pred[g] = jnp.zeros_like(pred[g])

        def body(h, _):
            if d:
                send4(g, h, d, b).wait_recv()
            c = columns(h, lax.rem(major(h) + SIDE - d, SIDE), b)
            high, low = parts(fit[g, :, c])
            both = dot(jnp.concatenate([high, low], 0), dh[:, c], 1, 1)
            pred[g] += both[:m] + both[m:] + dot(high, dl[:, c], 1, 1)
            return 0

        lax.fori_loop(0, 2, body, 0)

    def spread_sent(g):
        for h in range(2):
            for d in range(1, SIDE):
                for b in range(len(BLOCKS)):
                    send3(g, h, d, b).wait_send()
                    send4(g, h, d, b).wait_send()

    def scatter_pred(g):
        for k in far_first(peers):
            sendx1(g, k).start()

    def influence(g):
        for k in far_first(peers):
            sendx1(g, k).wait_recv()
        total = pred[g, piece_rows()]
        for k in range(1, peers):
            total = total + r3[g, k - 1]
        residual = total - targets[...]
        w = wt[pl.ds(pl.multiple_of(g * m + me * piece, 8), piece)]
        infl[g, piece_rows()] = w * residual / jnp.sqrt(1.0 + residual * residual)
        for k in far_first(peers):
            sendx2(g, k).start()
        for k in far_first(peers):
            sendx1(g, k).wait_send()

    steps[...] = jnp.broadcast_to(step_size[...], (members, members)).T
    counts_in.wait()
    wt[...] = kin[...].astype(F32).T
    wtb[...] = wt[...].astype(BF16)
    coef_in.wait()
    acc[...] = jnp.zeros_like(acc)

    def first_chunk(i, _):
        load(i).wait()
        c = pl.ds(pl.multiple_of(i * width, 128), width)
        high, low = parts(raw[:, c])
        dh[:, c] = high
        dl[:, c] = low
        fh, fl = parts(cin[c, :])
        both = dot(high, jnp.concatenate([fh, fl], 1))
        acc[...] += both[:, :members] + both[:, members:] + dot(low, fh)
        return 0

    lax.fori_loop(0, LOADS, first_chunk, 0)
    flipped = acc[...].T
    for g in range(GROUPS):
        pred[g] = flipped[g * m : (g + 1) * m]
    pl.semaphore_wait(barrier, 2 * (SIDE - 1) + peers - 1)
    for g in range(GROUPS):
        scatter_pred(g)

    def curve_part(d):
        def body(h, _):
            c = columns(h, lax.rem(major(h) + d, SIDE))
            x = raw[:, c]
            high, low = parts(x * x)
            curve[:, c] = dot(wtb[...], high) + dot(wtb[...], low)
            if d:
                sendk1(h, d).start()
            return 0

        lax.fori_loop(0, 2, body, 0)

    def curve_sum(h):
        for d in range(1, SIDE):
            sendk1(h, d).wait_recv()
        total = (curve[:, columns(h, major(h))] + c1[h, 0]) + (c1[h, 1] + c1[h, 2])
        for g in range(GROUPS):
            sc[h, g] = total[g * m : (g + 1) * m]
        for d in (2, 1, 3):
            sendk2(h, d).start()

    def curve_rate():
        for h in range(2):
            for d in range(1, SIDE):
                sendk2(h, d).wait_recv()
            for g in range(GROUPS):
                total = (sc[h, g, share_rows(h)] + c2[h, 0, g]) + (c2[h, 1, g] + c2[h, 2, g])
                mine = pl.ds(pl.multiple_of(g * m + minor(h) * part, 8), part)
                rate[g, h] = steps[mine, 0:1] / (total + 0.01)
        for h in range(2):
            for d in range(1, SIDE):
                sendk1(h, d).wait_send()
                sendk2(h, d).wait_send()

    curve_part(2)
    curve_part(1)
    influence(0)
    curve_part(3)
    curve_part(0)
    for h in range(2):
        start = pl.multiple_of(h * half + major(h) * quarter, 128)
        own = cin[pl.ds(start, quarter), :].T
        for g in range(GROUPS):
            fit[g, :, columns(h, major(h))] = own[g * m : (g + 1) * m]

    stages = dict(
        X3=gathered, G=gradients, P2=reduce1, P3=update, P4=spread, F=predict, KS=curve_sum, KR=curve_rate
    )

    def run(token):
        if token[0] == "K":
            name, where = token[1:3], token[3:]
            args = [int(v) for v in where]
        else:
            g = "AB".index(token[0])
            name = token[1:2] if token[1] in "GF" else token[1:3]
            args = [g] + [int(v) for v in token[1 + len(name) :]]
        if name == "X1":
            spread_sent(*args)
            scatter_pred(*args)
        elif name == "X2":
            influence(*args)
        else:
            stages[name](*args)

    turn = ORDER.index("BX3")

    def guard(i):
        token = ORDER[i]
        if token[0] == "K":
            return "first"
        if token[0] == "B" and i < turn:
            return "always" if token == "BX2" else "later"
        return "more" if token[1] == "F" or token[1:] in ("X1", "X2") else "always"

    def step(s, _):
        tests = dict(first=s == 0, later=s > 0, more=s < STEPS - 1)
        i = 0
        while i < len(ORDER):
            kind, j = guard(i), i
            while j < len(ORDER) and guard(j) == kind:
                j += 1

            def stretch(i=i, j=j):
                for token in ORDER[i:j]:
                    run(token)

            if kind == "always":
                stretch()
            else:
                pl.when(tests[kind])(stretch)
            i = j
        return 0

    lax.fori_loop(0, STEPS, step, 0)
    for token in ORDER[:turn]:
        if token[0] == "B" and token[1] in "GP":
            run(token)

    inf_copy = pltpu.make_async_copy(infl, inf_out, in_sem.at[0])
    inf_copy.start()

    def out_copy(g, h, d):
        c = columns(h, lax.rem(major(h) + SIDE - d, SIDE))
        return pltpu.make_async_copy(fit.at[g, :, c], fit_out.at[g, :, c], out_sem.at[g, h, d])

    for g in range(GROUPS):
        for h in range(2):
            out_copy(g, h, 0).start()
            for d in range(1, SIDE):
                for b in range(len(BLOCKS)):
                    send4(g, h, d, b).wait_recv()
                out_copy(g, h, d).start()
    for g in range(GROUPS):
        spread_sent(g)
        for h in range(2):
            for d in range(SIDE):
                out_copy(g, h, d).wait()
    inf_copy.wait()


def shards(design, targets, counts, coefficients, step_size):
    rows, cols = design.shape
    members = coefficients.shape[1]
    m = members // GROUPS
    quarter = cols // (2 * SIDE)
    part = m // SIDE
    peers = lax.axis_size("basis")
    piece = m // peers
    vmem = pltpu.VMEM
    dma = pltpu.SemaphoreType.DMA
    gh = (GROUPS, 2, SIDE - 1)
    ghb = (*gh, len(BLOCKS))
    any_spec = pl.BlockSpec(memory_space=pl.ANY)
    vmem_spec = pl.BlockSpec(memory_space=pltpu.VMEM)
    fit, infl = pl.pallas_call(
        kernel,
        out_shape=(
            jax.ShapeDtypeStruct((GROUPS, m, cols), F32),
            jax.ShapeDtypeStruct((GROUPS, m, rows), F32),
        ),
        in_specs=[any_spec, any_spec, any_spec, vmem_spec, vmem_spec],
        out_specs=(any_spec, any_spec),
        scratch_shapes=[
            vmem((members, members), F32),
            vmem((rows, cols), F32),
            vmem((rows, cols), BF16),
            vmem((rows, cols), BF16),
            vmem((cols, members), F32),
            vmem((rows, members), jnp.int32),
            vmem((members, rows), F32),
            vmem((members, rows), BF16),
            vmem((rows, members), F32),
            vmem((members, cols), F32),
            vmem((GROUPS, 2 * m, rows), BF16),
            vmem((GROUPS, m, cols), F32),
            vmem((GROUPS, m, cols), F32),
            vmem((GROUPS, m, rows), F32),
            vmem((GROUPS, m, rows), F32),
            vmem((*gh, m, quarter), F32),
            vmem((GROUPS, 2, m, quarter), F32),
            vmem((*gh, part, quarter), F32),
            vmem((GROUPS, peers - 1, piece, rows), F32),
            vmem((GROUPS, 2, part, quarter), F32),
            vmem((2, SIDE - 1, members, quarter), F32),
            vmem((2, GROUPS, m, quarter), F32),
            vmem((2, SIDE - 1, GROUPS, part, quarter), F32),
            dma((LOADS,)),
            dma((2,)),
            dma((GROUPS, 2, SIDE)),
            *[dma(ghb) for _ in range(8)],
            *[dma((GROUPS, peers - 1)) for _ in range(4)],
            *[dma((2, SIDE - 1)) for _ in range(4)],
        ],
        compiler_params=pltpu.CompilerParams(
            collective_id=0, has_side_effects=True, vmem_limit_bytes=60 * 2**20
        ),
    )(design, coefficients, counts, targets[None, :], step_size[None, :])
    return fit.reshape(members, cols).T, infl.reshape(members, rows).T


def solution(mesh):
    return jax.shard_map(
        shards,
        mesh=mesh,
        in_specs=(P("row", "basis"), P("row"), P("row", None), P("basis", None), P()),
        out_specs=(P("basis", None), P("row", None)),
        check_vma=False,
    )
```

```python
import functools

import jax
import jax.numpy as jnp
from jax import lax
from jax.experimental import pallas as pl
from jax.experimental.pallas import tpu as pltpu
from jax.sharding import PartitionSpec as P

STEPS = 3
SIDE = 4
LOADS = 8
GROUPS = 2
BLOCKS = (256, 384)
ORDER = (
    "AX3", "AG21", "AG11", "AG31", "BX2", "AG20", "AG01", "AG10", "AG30", "KKS0", "KKS1", "AP211", "AP201",
    "BX3", "BG20", "BG10", "BG30", "AG00", "AP210", "AP200", "BG21", "BG00", "BG11", "BG31", "KKR",
    "BP200", "BP210", "AP310", "AP300", "AP301", "AP311", "BG01", "BP201", "BP211", "BP310", "BP300",
    "AP410", "AP400", "AF00", "AP411", "BP301", "AP401", "BP311", "BP410", "AF01", "BP400", "BF00", "AF20",
    "AF10", "AF30", "AF21", "AF31", "BP401", "BP411", "AF11", "AX1", "BF01", "BF10", "BF30", "BF21",
    "BF11", "AX2", "BF31", "BF20", "BX1",
)
MESH = pl.DeviceIdType.MESH
F32 = jnp.float32
BF16 = jnp.bfloat16


def dot(a, b, ca=1, cb=0):
    return lax.dot_general(a, b, (((ca,), (cb,)), ((), ())), preferred_element_type=F32)


def far_first(n):
    return [k for k in (4, 5, 3, 2, 6, 1, 7) if k < n]


def parts(x):
    high = x.astype(BF16)
    return high, (x - high.astype(F32)).astype(BF16)


def kernel(
    design, coef, counts, targets, step_size, fit_out, inf_out,
    steps, raw, dh, dl, cin, kin, wt, wtb, acc, curve, icat,
    grad, fit, infl, pred, r1, s1, r2, r3, rate, c1, sc, c2,
    load_sem, in_sem, out_sem,
    p1s, p1r, p2s, p2r, p3s, p3r, p4s, p4r, x1s, x1r, x2s, x2r, k1s, k1r, k2s, k2r,
):
    rows, cols = raw.shape
    members = wt.shape[0]
    m = members // GROUPS
    quarter = cols // (2 * SIDE)
    half = cols // 2
    part = m // SIDE
    peers = lax.axis_size("basis")
    piece = m // peers
    row, me = lax.axis_index("row"), lax.axis_index("basis")
    y, z = row // SIDE, lax.rem(row, SIDE)

    def at_y(d):
        return (lax.rem(y + d, SIDE) * SIDE + z, me)

    def at_z(d):
        return (y * SIDE + lax.rem(z + d, SIDE), me)

    def at_b(k):
        return (row, lax.rem(me + k, peers))

    def major(h):
        return y + h * (z - y)

    def minor(h):
        return z + h * (y - z)

    def inside(b):
        return slice(sum(BLOCKS[:b]), sum(BLOCKS[: b + 1]))

    def columns(h, q, b=None):
        w = slice(0, quarter) if b is None else inside(b)
        return pl.ds(pl.multiple_of(h * half + q * quarter + w.start, 128), w.stop - w.start)

    def share_rows(h, d=0):
        return pl.ds(pl.multiple_of(lax.rem(minor(h) + d, SIDE) * part, 8), part)

    def piece_rows(k=0):
        return pl.ds(pl.multiple_of(lax.rem(me + k, peers) * piece, 8), piece)

    def remote(src, dst, send, recv, to):
        return pltpu.make_async_remote_copy(
            src_ref=src, dst_ref=dst, send_sem=send, recv_sem=recv, device_id=to, device_id_type=MESH
        )

    width = cols // LOADS

    def load(i):
        c = pl.ds(pl.multiple_of(i * width, 128), width)
        return pltpu.make_async_copy(design.at[:, c], raw.at[:, c], load_sem.at[i])

    coef_in = pltpu.make_async_copy(coef, cin, in_sem.at[0])
    counts_in = pltpu.make_async_copy(counts, kin, in_sem.at[1])
    counts_in.start()
    coef_in.start()
    for i in range(LOADS):
        load(i).start()

    barrier = pltpu.get_barrier_semaphore()
    for d in range(1, SIDE):
        pl.semaphore_signal(barrier, inc=1, device_id=at_y(d), device_id_type=MESH)
        pl.semaphore_signal(barrier, inc=1, device_id=at_z(d), device_id_type=MESH)
    for k in range(1, peers):
        pl.semaphore_signal(barrier, inc=1, device_id=at_b(k), device_id_type=MESH)

    def first(h, d):
        return (lax.rem(y + d * (1 - h), SIDE) * SIDE + lax.rem(z + d * h, SIDE), me)

    def second(h, d):
        return first(1 - h, d)

    def send1(g, h, d, b):
        c = columns(h, lax.rem(major(h) + d, SIDE), b)
        return remote(
            grad.at[g, :, c], r1.at[g, h, d - 1, :, inside(b)],
            p1s.at[g, h, d - 1, b], p1r.at[g, h, d - 1, b], first(h, d),
        )

    def send2(g, h, d, b):
        return remote(
            s1.at[g, h, share_rows(h, d), inside(b)], r2.at[g, h, d - 1, :, inside(b)],
            p2s.at[g, h, d - 1, b], p2r.at[g, h, d - 1, b], second(h, d),
        )

    def send3(g, h, d, b):
        mine = fit.at[g, share_rows(h), columns(h, major(h), b)]
        return remote(mine, mine, p3s.at[g, h, d - 1, b], p3r.at[g, h, d - 1, b], second(h, d))

    def send4(g, h, d, b):
        mine = fit.at[g, :, columns(h, major(h), b)]
        return remote(mine, mine, p4s.at[g, h, d - 1, b], p4r.at[g, h, d - 1, b], first(h, d))

    def sendx1(g, k):
        return remote(
            pred.at[g, piece_rows(k)], r3.at[g, k - 1], x1s.at[g, k - 1], x1r.at[g, k - 1], at_b(k)
        )

    def sendx2(g, k):
        mine = infl.at[g, piece_rows()]
        return remote(mine, mine, x2s.at[g, k - 1], x2r.at[g, k - 1], at_b(k))

    def sendk1(h, d):
        return remote(
            curve.at[:, columns(h, lax.rem(major(h) + d, SIDE))], c1.at[h, d - 1],
            k1s.at[h, d - 1], k1r.at[h, d - 1], first(h, d),
        )

    def sendk2(h, d):
        return remote(
            sc.at[h, :, share_rows(h, d)], c2.at[h, d - 1],
            k2s.at[h, d - 1], k2r.at[h, d - 1], second(h, d),
        )

    def gathered(g):
        for k in far_first(peers):
            sendx2(g, k).wait_recv()
        for k in far_first(peers):
            sendx2(g, k).wait_send()
        high, low = parts(infl[g])
        icat[g, 0:m] = high
        icat[g, m:] = low

    def gradients(g, d, b):
        def body(h, _):
            c = columns(h, lax.rem(major(h) + d, SIDE), b)
            both = dot(icat[g], dh[:, c])
            grad[g, :, c] = both[:m] + both[m:] + dot(icat[g, 0:m], dl[:, c])
            if d:
                send1(g, h, d, b).start()
            return 0

        lax.fori_loop(0, 2, body, 0)

    def reduce1(g, h, b):
        for d in range(1, SIDE):
            send1(g, h, d, b).wait_recv()
        w = inside(b)
        mine = grad[g, :, columns(h, major(h), b)]
        s1[g, h, :, w] = (mine + r1[g, h, 0, :, w]) + (r1[g, h, 1, :, w] + r1[g, h, 2, :, w])
        for d in (2, 1, 3):
            send2(g, h, d, b).start()

    def update(g, h, b):
        for d in range(1, SIDE):
            send2(g, h, d, b).wait_recv()
        w = inside(b)
        total = (s1[g, h, share_rows(h), w] + r2[g, h, 0, :, w]) + (r2[g, h, 1, :, w] + r2[g, h, 2, :, w])
        c = columns(h, major(h), b)
        fit[g, share_rows(h), c] = fit[g, share_rows(h), c] - total * rate[g, h, :, w]
        for d in (2, 1, 3):
            send3(g, h, d, b).start()
        for d in range(1, SIDE):
            send1(g, h, d, b).wait_send()

    def spread(g, h, b):
        for d in range(1, SIDE):
            send3(g, h, d, b).wait_recv()
        for d in (2, 1, 3):
            send4(g, h, d, b).start()
        for d in range(1, SIDE):
            send2(g, h, d, b).wait_send()

    def predict(g, d, b):
        if d == 0 and b == 0:
            pred[g] = jnp.zeros_like(pred[g])

        def body(h, _):
            if d:
                send4(g, h, d, b).wait_recv()
            c = columns(h, lax.rem(major(h) + SIDE - d, SIDE), b)
            high, low = parts(fit[g, :, c])
            both = dot(jnp.concatenate([high, low], 0), dh[:, c], 1, 1)
            pred[g] += both[:m] + both[m:] + dot(high, dl[:, c], 1, 1)
            return 0

        lax.fori_loop(0, 2, body, 0)

    def spread_sent(g):
        for h in range(2):
            for d in range(1, SIDE):
                for b in range(len(BLOCKS)):
                    send3(g, h, d, b).wait_send()
                    send4(g, h, d, b).wait_send()

    def scatter_pred(g):
        for k in far_first(peers):
            sendx1(g, k).start()

    def influence(g):
        for k in far_first(peers):
            sendx1(g, k).wait_recv()
        total = pred[g, piece_rows()]
        for k in range(1, peers):
            total = total + r3[g, k - 1]
        residual = total - targets[...]
        w = wt[pl.ds(pl.multiple_of(g * m + me * piece, 8), piece)]
        infl[g, piece_rows()] = w * residual / jnp.sqrt(1.0 + residual * residual)
        for k in far_first(peers):
            sendx2(g, k).start()
        for k in far_first(peers):
            sendx1(g, k).wait_send()

    steps[...] = jnp.broadcast_to(step_size[...], (members, members)).T
    counts_in.wait()
    wt[...] = kin[...].astype(F32).T
    wtb[...] = wt[...].astype(BF16)
    coef_in.wait()
    acc[...] = jnp.zeros_like(acc)

    def first_chunk(i, _):
        load(i).wait()
        c = pl.ds(pl.multiple_of(i * width, 128), width)
        high, low = parts(raw[:, c])
        dh[:, c] = high
        dl[:, c] = low
        fh, fl = parts(cin[c, :])
        both = dot(high, jnp.concatenate([fh, fl], 1))
        acc[...] += both[:, :members] + both[:, members:] + dot(low, fh)
        return 0

    lax.fori_loop(0, LOADS, first_chunk, 0)
    flipped = acc[...].T
    for g in range(GROUPS):
        pred[g] = flipped[g * m : (g + 1) * m]
    pl.semaphore_wait(barrier, 2 * (SIDE - 1) + peers - 1)
    for g in range(GROUPS):
        scatter_pred(g)

    def curve_part(d):
        def body(h, _):
            c = columns(h, lax.rem(major(h) + d, SIDE))
            x = raw[:, c]
            high, low = parts(x * x)
            curve[:, c] = dot(wtb[...], high) + dot(wtb[...], low)
            if d:
                sendk1(h, d).start()
            return 0

        lax.fori_loop(0, 2, body, 0)

    def curve_sum(h):
        for d in range(1, SIDE):
            sendk1(h, d).wait_recv()
        total = (curve[:, columns(h, major(h))] + c1[h, 0]) + (c1[h, 1] + c1[h, 2])
        for g in range(GROUPS):
            sc[h, g] = total[g * m : (g + 1) * m]
        for d in (2, 1, 3):
            sendk2(h, d).start()

    def curve_rate():
        for h in range(2):
            for d in range(1, SIDE):
                sendk2(h, d).wait_recv()
            for g in range(GROUPS):
                total = (sc[h, g, share_rows(h)] + c2[h, 0, g]) + (c2[h, 1, g] + c2[h, 2, g])
                mine = pl.ds(pl.multiple_of(g * m + minor(h) * part, 8), part)
                rate[g, h] = steps[mine, 0:1] / (total + 0.01)
        for h in range(2):
            for d in range(1, SIDE):
                sendk1(h, d).wait_send()
                sendk2(h, d).wait_send()

    curve_part(2)
    curve_part(1)
    influence(0)
    curve_part(3)
    curve_part(0)
    for h in range(2):
        start = pl.multiple_of(h * half + major(h) * quarter, 128)
        own = cin[pl.ds(start, quarter), :].T
        for g in range(GROUPS):
            fit[g, :, columns(h, major(h))] = own[g * m : (g + 1) * m]

    stages = dict(
        X3=gathered, G=gradients, P2=reduce1, P3=update, P4=spread, F=predict, KS=curve_sum, KR=curve_rate
    )

    def run(token):
        if token[0] == "K":
            name, where = token[1:3], token[3:]
            args = [int(v) for v in where]
        else:
            g = "AB".index(token[0])
            name = token[1:2] if token[1] in "GF" else token[1:3]
            args = [g] + [int(v) for v in token[1 + len(name) :]]
        if name == "X1":
            scatter_pred(*args)
            spread_sent(*args)
        elif name == "X2":
            influence(*args)
        else:
            stages[name](*args)

    turn = ORDER.index("BX3")

    def guard(i):
        token = ORDER[i]
        if token[0] == "K":
            return "first"
        if token[0] == "B" and i < turn:
            return "always" if token == "BX2" else "later"
        return "more" if token[1] == "F" or token[1:] in ("X1", "X2") else "always"

    def step(s, _):
        tests = dict(first=s == 0, later=s > 0, more=s < STEPS - 1)
        i = 0
        while i < len(ORDER):
            kind, j = guard(i), i
            while j < len(ORDER) and guard(j) == kind:
                j += 1

            def stretch(i=i, j=j):
                for token in ORDER[i:j]:
                    run(token)

            if kind == "always":
                stretch()
            else:
                pl.when(tests[kind])(stretch)
            i = j
        return 0

    lax.fori_loop(0, STEPS, step, 0)
    for token in ORDER[:turn]:
        if token[0] == "B" and token[1] in "GP":
            run(token)

    inf_copy = pltpu.make_async_copy(infl, inf_out, in_sem.at[0])
    inf_copy.start()

    def out_copy(g, h, d):
        c = columns(h, lax.rem(major(h) + SIDE - d, SIDE))
        return pltpu.make_async_copy(fit.at[g, :, c], fit_out.at[g, :, c], out_sem.at[g, h, d])

    for g in range(GROUPS):
        for h in range(2):
            out_copy(g, h, 0).start()
            for d in range(1, SIDE):
                for b in range(len(BLOCKS)):
                    send4(g, h, d, b).wait_recv()
                out_copy(g, h, d).start()
    for g in range(GROUPS):
        spread_sent(g)
        for h in range(2):
            for d in range(SIDE):
                out_copy(g, h, d).wait()
    inf_copy.wait()


def shards(design, targets, counts, coefficients, step_size):
    rows, cols = design.shape
    members = coefficients.shape[1]
    m = members // GROUPS
    quarter = cols // (2 * SIDE)
    part = m // SIDE
    peers = lax.axis_size("basis")
    piece = m // peers
    vmem = pltpu.VMEM
    dma = pltpu.SemaphoreType.DMA
    gh = (GROUPS, 2, SIDE - 1)
    ghb = (*gh, len(BLOCKS))
    any_spec = pl.BlockSpec(memory_space=pl.ANY)
    vmem_spec = pl.BlockSpec(memory_space=pltpu.VMEM)
    fit, infl = pl.pallas_call(
        kernel,
        out_shape=(
            jax.ShapeDtypeStruct((GROUPS, m, cols), F32),
            jax.ShapeDtypeStruct((GROUPS, m, rows), F32),
        ),
        in_specs=[any_spec, any_spec, any_spec, vmem_spec, vmem_spec],
        out_specs=(any_spec, any_spec),
        scratch_shapes=[
            vmem((members, members), F32),
            vmem((rows, cols), F32),
            vmem((rows, cols), BF16),
            vmem((rows, cols), BF16),
            vmem((cols, members), F32),
            vmem((rows, members), jnp.int32),
            vmem((members, rows), F32),
            vmem((members, rows), BF16),
            vmem((rows, members), F32),
            vmem((members, cols), F32),
            vmem((GROUPS, 2 * m, rows), BF16),
            vmem((GROUPS, m, cols), F32),
            vmem((GROUPS, m, cols), F32),
            vmem((GROUPS, m, rows), F32),
            vmem((GROUPS, m, rows), F32),
            vmem((*gh, m, quarter), F32),
            vmem((GROUPS, 2, m, quarter), F32),
            vmem((*gh, part, quarter), F32),
            vmem((GROUPS, peers - 1, piece, rows), F32),
            vmem((GROUPS, 2, part, quarter), F32),
            vmem((2, SIDE - 1, members, quarter), F32),
            vmem((2, GROUPS, m, quarter), F32),
            vmem((2, SIDE - 1, GROUPS, part, quarter), F32),
            dma((LOADS,)),
            dma((2,)),
            dma((GROUPS, 2, SIDE)),
            *[dma(ghb) for _ in range(8)],
            *[dma((GROUPS, peers - 1)) for _ in range(4)],
            *[dma((2, SIDE - 1)) for _ in range(4)],
        ],
        compiler_params=pltpu.CompilerParams(
            collective_id=0, has_side_effects=True, vmem_limit_bytes=60 * 2**20
        ),
    )(design, coefficients, counts, targets[None, :], step_size[None, :])
    return fit.reshape(members, cols).T, infl.reshape(members, rows).T


def solution(mesh):
    return jax.shard_map(
        shards,
        mesh=mesh,
        in_specs=(P("row", "basis"), P("row"), P("row", None), P("basis", None), P()),
        out_specs=(P("basis", None), P("row", None)),
        check_vma=False,
    )
```
